128 devices in a mesh: fac: 32 (over y, x, z_hi), loc: 4 (over z_lo, core).
Axes of the slice: x: 4, y: 4, z: 4 (z_hi: 2, z_lo: 2; z = z_hi * 2 + z_lo), core: 2. Of those that a mesh axis runs over, the one named last changes fastest.
Arguments:
- quad_cost: float32 [128, 128, 128, 128], P('fac', 'loc'), may hold values from -30 to 30
- leader: float32 [128, 128], P('fac', 'loc'), may hold values from -4 to 4
Outputs:
- new_cost: float32 [128, 128, 128, 128], P('fac', 'loc')
- new_leader: float32 [128, 128], P('fac', 'loc')
The draws below stay inside these ranges and needn't reach their ends.
All inputs are finite; a program needn't handle non-finite values.
Results may differ from the reference program's by a relative error of at most 0.0001.
Values sent between devices are 32-bit elements; how exact they have to be, the bound alone decides.
No kernel may reach another device: no remote copies, remote signals or barrier semaphores. Data moves between devices by JAX's collectives and lax.ppermute only.
A program may use at most 192 MiB of HBM per device.

```python
import math
import jax
import jax.numpy as jnp
from jax import lax

N = 128
SWEEPS = 3
UPDATES = 1


def draw_quad_cost(key, part):
    key_base = jax.random.fold_in(key, 101)
    key_row = jax.random.fold_in(key, 103)
    key_col = jax.random.fold_in(key, 104)
    base = jnp.clip(jax.random.normal(key_base, (N, N, N, N), jnp.float32), -4.0, 4.0)
    row_scale = jnp.exp(jax.random.uniform(key_row, (N, N, N, 1), jnp.float32, 0.0, math.log(3.0)))
    col_scale = jnp.exp(jax.random.uniform(key_col, (N, N, 1, N), jnp.float32, 0.0, math.log(2.0)))
    return base * row_scale * col_scale


def levels(rng, shape, pieces, low, high):
    gain, own = 1.0, jax.random.fold_in(rng, 6)
    for axis_at, blocks in pieces:
        steps = jnp.exp(jax.random.uniform(jax.random.fold_in(own, axis_at), (blocks,), jnp.float32, low / len(pieces), high / len(pieces)))
        gain = gain * jnp.repeat(steps, shape[axis_at] // blocks).reshape([-1 if axis == axis_at else 1 for axis in range(len(shape))])
    return gain


def scatter_about(key, dims, deviation, reach, pieces=(), held_as=jnp.bfloat16):
    result = deviation * jax.random.normal(key, dims, jnp.float32)
    if pieces:
        result = result * levels(key, dims, pieces, -0.22, 0.18)
    return jnp.clip(result, -reach, reach).astype(held_as)


def setup_inputs(seed: int = 0) -> dict:
    streams_of = jax.random.split(jax.random.key(seed), 3)
    return {
        "quad_cost": draw_quad_cost(jax.random.fold_in(streams_of[2], 71), 0),
        "leader": scatter_about(streams_of[1], (N, N), 1.0, 4.0, ((0, 32), (1, 4)), jnp.float32),
    }


temper = 0.15
leader_temper = 0.1


def soft_min(values, axis, scale):
    scaled = -values / scale
    highest = jnp.max(scaled, axis=axis, keepdims=True)
    totals = jnp.sum(jnp.exp(scaled - highest), axis=axis, keepdims=True)
    return jnp.squeeze(-scale * (highest + jnp.log(totals)), axis)


def sweep_block(block):
    col_dual = jnp.zeros(block.shape[:-2] + (block.shape[-1],), jnp.float32)
    row_dual = jnp.zeros(block.shape[:-1], jnp.float32)
    for sweep in range(SWEEPS):
        row_dual = soft_min(block - col_dual[..., None, :], -1, temper)
        col_dual = soft_min(block - row_dual[..., :, None], -2, temper)
    reduced = block - row_dual[..., :, None] - col_dual[..., None, :]
    worth = (jnp.sum(row_dual, -1) + jnp.sum(col_dual, -1)) / N
    return reduced, worth


def reference(quad_cost, leader):
    for update in range(UPDATES):
        reduced, worth = lax.map(sweep_block, quad_cost)
        partner = jnp.transpose(reduced, (2, 3, 0, 1))
        quad_cost = 0.5 * (reduced + partner)
        leader = leader + worth
        leader = leader - soft_min(leader, 1, leader_temper)[:, None]
        leader = leader - soft_min(leader, 0, leader_temper)[None, :]
    return quad_cost, leader
```

```python
import jax
import jax.numpy as jnp
from jax import lax
from jax.experimental import pallas as pl
from jax.experimental.pallas import tpu as pltpu
from jax.sharding import PartitionSpec as P

N = 128
FAC = 32
LOC = 4
FR = N // FAC
LR = N // LOC

temper = 0.15
leader_temper = 0.1
LOG2E = 1.4426950408889634
INNER = LOG2E / temper
UNROLL = 2


def over_groups(x, combine):
    x = combine(x, pltpu.roll(x, LR, 1))
    return combine(x, pltpu.roll(x, 2 * LR, 1))


def sweep_kernel(c_ref, s_ref, u_ref, v_ref, w_ref, d_ref, e_ref, m_ref, a_ref):
    def load(f, col_min):
        rows = [c_ref[pl.ds(FR * f + k, LR, stride=N), :] for k in range(FR)]
        x = jnp.concatenate(rows, 0).T
        row_min = jnp.min(x, 0, keepdims=True)
        x = x - row_min
        d_ref[f] = x
        m_ref[pl.ds(f, 1), :] = row_min
        return jnp.minimum(col_min, x)

    col_min = lax.fori_loop(0, FAC, load, jnp.full((N, N), jnp.inf, jnp.float32), unroll=UNROLL)
    col_min = over_groups(col_min, jnp.minimum)

    weight = jnp.exp2(-INNER * col_min)

    def first(f, total):
        e = jnp.exp2(INNER * (col_min - d_ref[f]))
        e_ref[f] = e
        a = 1.0 / jnp.sum(e * weight, 0, keepdims=True)
        return total + e * a

    zero = jnp.zeros((N, N), jnp.float32)
    b = 1.0 / over_groups(lax.fori_loop(0, FAC, first, zero, unroll=UNROLL), jnp.add)

    for _ in range(2):

        def later(f, total, b=b):
            e = e_ref[f]
            a = 1.0 / jnp.sum(e * b, 0, keepdims=True)
            a_ref[pl.ds(f, 1), :] = a
            return total + e * a

        b = 1.0 / over_groups(lax.fori_loop(0, FAC, later, zero, unroll=UNROLL), jnp.add)

    row_part = temper * jnp.log(a_ref[...])
    a_ref[...] = row_part
    col = col_min + temper * jnp.log(b)

    def emit(f, carry):
        r = d_ref[f] - col - a_ref[pl.ds(f, 1), :]
        s_ref[pl.ds(f * LOC, LOC), :, :] = r.reshape(LOC, LR, N)
        return carry

    lax.fori_loop(0, FAC, emit, 0, unroll=UNROLL)
    row = m_ref[...] + row_part
    u_ref[...] = jnp.concatenate([row, jnp.zeros((N - FAC, N), jnp.float32)], 0).T
    v_ref[...] = col.T[:LR]
    worth = over_groups(jnp.sum(row, 0, keepdims=True), jnp.add) + jnp.sum(col, 0, keepdims=True)
    w_ref[...] = worth * (1.0 / N)


def sweeps(quad_cost):
    rows = LR * N
    return pl.pallas_call(
        sweep_kernel,
        grid=(FR,),
        in_specs=[pl.BlockSpec((rows, N), lambda i: (i, 0))],
        out_specs=[
            pl.BlockSpec((FAC * LOC, None, LR, N), lambda i: (0, i, 0, 0)),
            pl.BlockSpec((None, N, N), lambda i: (i, 0, 0)),
            pl.BlockSpec((None, LR, N), lambda i: (i, 0, 0)),
            pl.BlockSpec((None, 1, N), lambda i: (i, 0, 0)),
        ],
        out_shape=[
            jax.ShapeDtypeStruct((FAC * LOC, FR, LR, N), jnp.float32),
            jax.ShapeDtypeStruct((FR, N, N), jnp.float32),
            jax.ShapeDtypeStruct((FR, LR, N), jnp.float32),
            jax.ShapeDtypeStruct((FR, 1, N), jnp.float32),
        ],
        scratch_shapes=[
            pltpu.VMEM((FAC, N, N), jnp.float32),
            pltpu.VMEM((FAC, N, N), jnp.float32),
            pltpu.VMEM((FAC, N), jnp.float32),
            pltpu.VMEM((FAC, N), jnp.float32),
        ],
    )(quad_cost.reshape(FR * rows, N))


def regroup(parts):
    lane = lax.broadcasted_iota(jnp.int32, parts[0].shape, 1)
    low = lane < 2 * LR
    p0, p1, p2, p3 = parts
    q0 = jnp.where(low, p0, pltpu.roll(p2, 2 * LR, 1))
    q2 = jnp.where(low, pltpu.roll(p0, 2 * LR, 1), p2)
    q1 = jnp.where(low, p1, pltpu.roll(p3, 2 * LR, 1))
    q3 = jnp.where(low, pltpu.roll(p1, 2 * LR, 1), p3)
    even = (lane & LR) == 0
    return [
        jnp.where(even, q0, pltpu.roll(q1, LR, 1)),
        jnp.where(even, pltpu.roll(q0, 3 * LR, 1), q1),
        jnp.where(even, q2, pltpu.roll(q3, LR, 1)),
        jnp.where(even, pltpu.roll(q2, 3 * LR, 1), q3),
    ]


STEP = 8
STEP_F = STEP // FR


def soft_min(values, axis, scale):
    scaled = -values / scale
    highest = jnp.max(scaled, axis=axis, keepdims=True)
    totals = jnp.sum(jnp.exp(scaled - highest), axis=axis, keepdims=True)
    return -scale * (highest + jnp.log(totals))


def join_kernel(place_ref, c_ref, r_ref, u_ref, v_ref, b_ref, o_ref, nb_ref, bs_ref):
    step = pl.program_id(0)
    c_rows = c_ref.reshape(FR * LR * STEP, N)
    o_rows = o_ref.reshape(FR * LR * STEP, N)

    @pl.when(step == 0)
    def _():
        b = regroup([b_ref[pl.ds(g, FAC, stride=LOC), :] for g in range(LOC)])
        b = [x - soft_min(x, 1, leader_temper) for x in b]
        b = jnp.concatenate(b, 0)
        bs_ref[...] = b - soft_min(b, 0, leader_temper)
        for i in range(FR):
            row = bs_ref[pl.ds(i * FAC + place_ref[0], 1), :]
            row = pltpu.roll(row, (LOC - place_ref[1]) * LR, 1)
            nb_ref[pl.ds(i, 1), :] = row[:, :LR]

    for g in range(STEP_F):
        f = step * STEP_F + g
        shift = lax.rem(N - f, N)
        for k in range(FR):
            for t in range(LR // 8):
                parts = [r_ref[g * LOC + s, k, pl.ds(t * 8, 8), :] for s in range(LOC)]
                parts = regroup(parts)
                for a in range(FR):
                    at = pl.ds((a * LR + t * 8) * STEP + g * FR + k, 8, stride=STEP)
                    row = u_ref[a, pl.ds(k * LR + t * 8, 8), :]
                    row = pltpu.roll(row, shift, 1)[:, :1]
                    own = c_rows[at, :] - row - v_ref[a, pl.ds(t * 8, 8), :]
                    o_rows[at, :] = 0.5 * (own + parts[a])


def join(quad_cost, incoming, row, col, leader, place):
    return pl.pallas_call(
        join_kernel,
        grid_spec=pltpu.PrefetchScalarGridSpec(
            num_scalar_prefetch=1,
            grid=(N // STEP,),
            in_specs=[
                pl.BlockSpec((FR, LR, STEP, N), lambda i, p: (0, 0, i, 0)),
                pl.BlockSpec((STEP_F * LOC, FR, LR, N), lambda i, p: (i, 0, 0, 0)),
                pl.BlockSpec((FR, N, N), lambda i, p: (0, 0, 0)),
                pl.BlockSpec((FR, LR, N), lambda i, p: (0, 0, 0)),
                pl.BlockSpec((N, N), lambda i, p: (0, 0)),
            ],
            out_specs=[
                pl.BlockSpec((FR, LR, STEP, N), lambda i, p: (0, 0, i, 0)),
                pl.BlockSpec((FR, LR), lambda i, p: (0, 0)),
            ],
            scratch_shapes=[pltpu.VMEM((N, N), jnp.float32)],
        ),
        out_shape=[
            jax.ShapeDtypeStruct((FR, LR, N, N), jnp.float32),
            jax.ShapeDtypeStruct((FR, LR), jnp.float32),
        ],
    )(place, quad_cost, incoming, row, col, leader)


def on_device(quad_cost, leader):
    send, row, col, worth = sweeps(quad_cost)
    leader = leader + worth[:, 0, :LR]
    incoming = lax.all_to_all(send, ("fac", "loc"), split_axis=0, concat_axis=0, tiled=True)
    everywhere = lax.all_gather(leader.reshape(1, N), ("fac", "loc"), tiled=True)
    place = jnp.stack([lax.axis_index("fac"), lax.axis_index("loc")]).astype(jnp.int32)
    quad_cost, leader = join(quad_cost, incoming, row, col, everywhere, place)
    return quad_cost, leader


def solution(mesh):
    return jax.shard_map(
        on_device,
        mesh=mesh,
        in_specs=(P("fac", "loc", None, None), P("fac", "loc")),
        out_specs=(P("fac", "loc", None, None), P("fac", "loc")),
        check_vma=False,
    )
```

```python
import jax
import jax.numpy as jnp
from jax import lax
from jax.experimental import pallas as pl
from jax.experimental.pallas import tpu as pltpu
from jax.sharding import PartitionSpec as P

N = 128
FAC = 32
LOC = 4
FR = N // FAC
LR = N // LOC

temper = 0.15
leader_temper = 0.1
LOG2E = 1.4426950408889634
INNER = LOG2E / temper
UNROLL = 8
DEVICES = FAC * LOC
PIECE = N + 1
STEP = 16
STEP_F = STEP // FR
VMEM_LIMIT = 60 << 20
AXES = ("fac", "loc")


def over_groups(x, combine):
    x = combine(x, pltpu.roll(x, LR, 1))
    return combine(x, pltpu.roll(x, 2 * LR, 1))


def sweep_kernel(c_ref, b_ref, s_ref, u_ref, v_ref, d_ref, e_ref, m_ref, a_ref, w_ref, out_ref, line_ref, sem, line_sem):
    slab = pl.program_id(0)
    slot = slab & 1
    loc = lax.axis_index("loc")

    def load(f, col_min):
        rows = []
        for g in range(LOC):
            k = (g + LOC - loc) & (LOC - 1)
            rows.append(c_ref[pl.ds(FR * f + k, LR, stride=N), :])
        x = jnp.concatenate(rows, 0).T
        row_min = jnp.min(x, 0, keepdims=True)
        x = x - row_min
        d_ref[f] = x
        m_ref[pl.ds(f, 1), :] = row_min
        return jnp.minimum(col_min, x)

    col_min = lax.fori_loop(0, FAC, load, jnp.full((N, N), jnp.inf, jnp.float32), unroll=UNROLL)
    col_min = over_groups(col_min, jnp.minimum)

    weight = jnp.exp2(-INNER * col_min)

    def first(f, total):
        e = jnp.exp2(INNER * (col_min - d_ref[f]))
        e_ref[f] = e
        a = 1.0 / jnp.sum(e * weight, 0, keepdims=True)
        return total + e * a

    zero = jnp.zeros((N, N), jnp.float32)
    b = 1.0 / over_groups(lax.fori_loop(0, FAC, first, zero, unroll=UNROLL), jnp.add)

    for _ in range(2):

        def later(f, total, b=b):
            e = e_ref[f]
            a = 1.0 / jnp.sum(e * b, 0, keepdims=True)
            a_ref[pl.ds(f, 1), :] = a
            return total + e * a

        b = 1.0 / over_groups(lax.fori_loop(0, FAC, later, zero, unroll=UNROLL), jnp.add)

    row_part = temper * jnp.log(a_ref[...])
    a_ref[...] = row_part
    col = col_min + temper * jnp.log(b)

    def slab_done(at):
        pltpu.make_async_copy(out_ref.at[at], s_ref.at[pl.ds(0, FAC * N)], sem.at[at]).wait()

    @pl.when(slab >= 2)
    def _():
        slab_done(slot)

    def ship(f):
        for s in range(LOC):
            pltpu.make_async_copy(
                out_ref.at[slot, pl.ds(f * N + s * LR, LR)],
                s_ref.at[pl.ds((f * LOC + s) * PIECE + slab * LR, LR)],
                sem.at[slot],
            ).start()

    def emit(f, carry):
        out_ref[slot, pl.ds(pl.multiple_of(f * N, N), N), :] = d_ref[f] - col - a_ref[pl.ds(f, 1), :]

        @pl.when(f > 0)
        def _():
            ship(f - 1)

        return carry

    lax.fori_loop(0, FAC, emit, 0, unroll=UNROLL)
    ship(FAC - 1)
    row = m_ref[...] + row_part
    u_ref[...] = jnp.concatenate([row, jnp.zeros((N - FAC, N), jnp.float32)], 0).T
    v_ref[...] = col.T[:LR]
    worth = over_groups(jnp.sum(row, 0, keepdims=True), jnp.add) + jnp.sum(col, 0, keepdims=True)
    w_ref[pl.ds(slab, 1), :] = worth * (1.0 / N)

    @pl.when(slab == FR - 1)
    def _():
        leader = jnp.concatenate([b_ref[...]] * LOC, 1) + w_ref[...]
        group = lax.broadcasted_iota(jnp.int32, (1, N), 1) // LR
        line = leader[:1]
        for i in range(FR):
            line = jnp.where(group == ((i + loc) & (LOC - 1)), leader[i : i + 1], line)
        line_ref[...] = line

        def send(d, carry):
            pltpu.make_async_copy(line_ref, s_ref.at[pl.ds(d * PIECE + N, 1)], line_sem).start()
            return carry

        lax.fori_loop(0, DEVICES, send, 0, unroll=8)

        pltpu.make_async_copy(out_ref.at[0, pl.ds(0, DEVICES)], s_ref.at[pl.ds(0, DEVICES)], line_sem).wait()
        slab_done(1 - slot)
        slab_done(slot)


def sweeps(quad_cost, leader):
    rows = LR * N
    return pl.pallas_call(
        sweep_kernel,
        grid=(FR,),
        in_specs=[
            pl.BlockSpec((rows, N), lambda i: (i, 0)),
            pl.BlockSpec((FR, LR), lambda i: (0, 0)),
        ],
        out_specs=[
            pl.BlockSpec(memory_space=pl.ANY),
            pl.BlockSpec((None, N, N), lambda i: (i, 0, 0)),
            pl.BlockSpec((None, LR, N), lambda i: (i, 0, 0)),
        ],
        out_shape=[
            jax.ShapeDtypeStruct((DEVICES * PIECE, N), jnp.float32),
            jax.ShapeDtypeStruct((FR, N, N), jnp.float32),
            jax.ShapeDtypeStruct((FR, LR, N), jnp.float32),
        ],
        scratch_shapes=[
            pltpu.VMEM((FAC, N, N), jnp.float32),
            pltpu.VMEM((FAC, N, N), jnp.float32),
            pltpu.VMEM((FAC, N), jnp.float32),
            pltpu.VMEM((FAC, N), jnp.float32),
            pltpu.VMEM((FR, N), jnp.float32),
            pltpu.VMEM((2, FAC * N, N), jnp.float32),
            pltpu.VMEM((1, N), jnp.float32),
            pltpu.SemaphoreType.DMA((2,)),
            pltpu.SemaphoreType.DMA,
        ],
        compiler_params=pltpu.CompilerParams(vmem_limit_bytes=VMEM_LIMIT),
    )(quad_cost.reshape(FR * rows, N), leader)


def own_kernel(c_ref, u_ref, v_ref, o_ref):
    step = pl.program_id(0)
    loc = lax.axis_index("loc")
    c_rows = c_ref.reshape(FR * LR * STEP, N)
    o_rows = o_ref.reshape(FR * LR * STEP, N)
    for g in range(STEP_F):
        shift = lax.rem(N - (step * STEP_F + g), N)
        for k in range(FR):
            begin = ((k + loc) & (FR - 1)) * LR
            for a in range(FR):
                row = u_ref[a, pl.ds(pl.multiple_of(begin, LR), LR), :]
                row = pltpu.roll(row, shift, 1)[:, :1]
                at = pl.ds(a * LR * STEP + g * FR + k, LR, stride=STEP)
                o_rows[at, :] = 0.5 * (c_rows[at, :] - row - v_ref[a])


def own_half(quad_cost, row, col):
    return pl.pallas_call(
        own_kernel,
        grid=(N // STEP,),
        in_specs=[
            pl.BlockSpec((FR, LR, STEP, N), lambda i: (0, 0, i, 0)),
            pl.BlockSpec((FR, N, N), lambda i: (0, 0, 0)),
            pl.BlockSpec((FR, LR, N), lambda i: (0, 0, 0)),
        ],
        out_specs=pl.BlockSpec((FR, LR, STEP, N), lambda i: (0, 0, i, 0)),
        out_shape=jax.ShapeDtypeStruct((FR, LR, N, N), jnp.float32),
        compiler_params=pltpu.CompilerParams(vmem_limit_bytes=VMEM_LIMIT),
        cost_estimate=pl.CostEstimate(flops=1 << 23, bytes_accessed=1 << 24, transcendentals=0),
    )(quad_cost, row, col)


def regroup(parts):
    group = lax.broadcasted_iota(jnp.int32, parts[0].shape, 1) // LR
    odd = (group & 1) == 1
    low = group < 2
    p0, p1, p2, p3 = parts
    even_a, even_b = jnp.where(odd, p1, p0), jnp.where(odd, p3, p2)
    odd_a, odd_b = jnp.where(odd, p0, p3), jnp.where(odd, p2, p1)
    return [
        jnp.where(low, even_a, even_b),
        pltpu.roll(jnp.where(low, odd_a, odd_b), 3 * LR, 1),
        pltpu.roll(jnp.where(low, even_b, even_a), 2 * LR, 1),
        pltpu.roll(jnp.where(low, odd_b, odd_a), LR, 1),
    ]


def soft_min(values, axis, scale):
    scaled = -values / scale
    highest = jnp.max(scaled, axis=axis, keepdims=True)
    totals = jnp.sum(jnp.exp(scaled - highest), axis=axis, keepdims=True)
    return -scale * (highest + jnp.log(totals))


def join_kernel(q_ref, r_ref, o_ref, nb_ref, in_ref, lead_ref, bs_ref, sem, lead_sem):
    step = pl.program_id(0)
    slot = step & 1
    sources = STEP_F * LOC

    def piece(at, n, to):
        return pltpu.make_async_copy(r_ref.at[pl.ds((at * sources + n) * PIECE, N)], in_ref.at[to, n], sem.at[to, n])

    def fetch(at, to):
        for n in range(sources):
            piece(at, n, to).start()

    def lead(d):
        return pltpu.make_async_copy(r_ref.at[pl.ds(d * PIECE + N, 1)], lead_ref.at[pl.ds(d, 1)], lead_sem)

    @pl.when(step == 0)
    def _():
        fetch(0, 0)

        def start(d, carry):
            lead(d).start()
            return carry

        lax.fori_loop(0, DEVICES, start, 0, unroll=8)

    @pl.when(step + 1 < pl.num_programs(0))
    def _():
        fetch(step + 1, 1 - slot)

    @pl.when(step == 1)
    def _():
        pltpu.make_async_copy(r_ref.at[pl.ds(0, DEVICES)], lead_ref, lead_sem).wait()
        fac, loc = (lax.axis_index(name) for name in AXES)
        b = regroup([lead_ref[pl.ds(g, FAC, stride=LOC), :] for g in range(LOC)])
        b = [x - soft_min(x, 1, leader_temper) for x in b]
        b = jnp.concatenate(b, 0)
        bs_ref[...] = b - soft_min(b, 0, leader_temper)
        for i in range(FR):
            row = bs_ref[pl.ds(i * FAC + fac, 1), :]
            row = pltpu.roll(row, (LOC - loc) * LR, 1)
            nb_ref[pl.ds(i, 1), :] = row[:, :LR]

    for n in range(sources):
        piece(step, n, slot).wait()
    q_rows = q_ref.reshape(FR * LR * STEP, N)
    o_rows = o_ref.reshape(FR * LR * STEP, N)
    for g in range(STEP_F):
        for k in range(FR):
            for t in range(LR // 8):
                parts = [in_ref[slot, g * LOC + s, pl.ds(k * LR + t * 8, 8), :] for s in range(LOC)]
                parts = regroup(parts)
                for a in range(FR):
                    at = pl.ds((a * LR + t * 8) * STEP + g * FR + k, 8, stride=STEP)
                    o_rows[at, :] = q_rows[at, :] + 0.5 * parts[a]


def join(own, incoming):
    return pl.pallas_call(
        join_kernel,
        grid=(N // STEP,),
        in_specs=[
            pl.BlockSpec((FR, LR, STEP, N), lambda i: (0, 0, i, 0)),
            pl.BlockSpec(memory_space=pl.ANY),
        ],
        out_specs=[
            pl.BlockSpec((FR, LR, STEP, N), lambda i: (0, 0, i, 0)),
            pl.BlockSpec((FR, LR), lambda i: (0, 0)),
        ],
        out_shape=[
            jax.ShapeDtypeStruct((FR, LR, N, N), jnp.float32),
            jax.ShapeDtypeStruct((FR, LR), jnp.float32),
        ],
        scratch_shapes=[
            pltpu.VMEM((2, STEP_F * LOC, N, N), jnp.float32),
            pltpu.VMEM((DEVICES, N), jnp.float32),
            pltpu.VMEM((N, N), jnp.float32),
            pltpu.SemaphoreType.DMA((2, STEP_F * LOC)),
            pltpu.SemaphoreType.DMA,
        ],
        compiler_params=pltpu.CompilerParams(vmem_limit_bytes=VMEM_LIMIT),
    )(own, incoming)


def on_device(quad_cost, leader):
    send, row, col = sweeps(quad_cost, leader)
    send = send.reshape(DEVICES, PIECE, 1, N)
    incoming = lax.all_to_all(send, AXES, split_axis=0, concat_axis=0, tiled=True)
    own = own_half(quad_cost, row, col)
    return tuple(join(own, incoming.reshape(DEVICES * PIECE, N)))


def solution(mesh):
    return jax.shard_map(
        on_device,
        mesh=mesh,
        in_specs=(P("fac", "loc", None, None), P("fac", "loc")),
        out_specs=(P("fac", "loc", None, None), P("fac", "loc")),
        check_vma=False,
    )
```

```python
import jax
import jax.numpy as jnp
from jax import lax
from jax.experimental import pallas as pl
from jax.experimental.pallas import tpu as pltpu
from jax.sharding import PartitionSpec as P

N = 128
FAC = 32
LOC = 4
FR = N // FAC
LR = N // LOC

temper = 0.15
leader_temper = 0.1
LOG2E = 1.4426950408889634
INNER = LOG2E / temper
UNROLL = 32
DEVICES = FAC * LOC
PIECE = N + 1
PITCH = N + 1
PARTS = 2
WIDTH = N // PARTS
STEP = 32
STEP_F = STEP // FR
SPACE = LR + 1
VMEM_LIMIT = 67043328
AXES = ("fac", "loc")


def over_groups(x, combine):
    x = combine(x, pltpu.roll(x, LR, 1))
    return combine(x, pltpu.roll(x, 2 * LR, 1))


def sweep_kernel(c_ref, b_ref, s_ref, u_ref, v_ref, d_ref, e_ref, m_ref, a_ref, w_ref, in_ref, out_ref, line_ref, in_sem, sem, line_sem):
    slab = pl.program_id(0)
    slot = slab & 1
    loc = lax.axis_index("loc")

    def fetch(at, to):
        for part in range(PARTS):
            for j in range(LR):
                pltpu.make_async_copy(
                    c_ref.at[pl.ds((at * LR + j) * N + part * WIDTH, WIDTH)],
                    in_ref.at[to, pl.ds(j * PITCH + part * WIDTH, WIDTH)],
                    in_sem.at[to, part],
                ).start()

    @pl.when(slab == 0)
    def _():
        fetch(0, 0)

    @pl.when(slab + 1 < FR)
    def _():
        fetch(slab + 1, 1 - slot)

    def load(f, col_min):
        rows = []
        for g in range(LOC):
            k = (g + LOC - loc) & (LOC - 1)
            rows.append(in_ref[slot, pl.ds(FR * f + k, LR, stride=PITCH), :])
        x = jnp.concatenate(rows, 0).T
        row_min = jnp.min(x, 0, keepdims=True)
        x = x - row_min
        d_ref[f] = x
        m_ref[pl.ds(f, 1), :] = row_min
        return jnp.minimum(col_min, x)

    col_min = jnp.full((N, N), jnp.inf, jnp.float32)
    for part in range(PARTS):
        pltpu.make_async_copy(
            c_ref.at[pl.ds(0, LR * WIDTH)], in_ref.at[slot, pl.ds(0, LR * WIDTH)], in_sem.at[slot, part]
        ).wait()
        col_min = lax.fori_loop(part * WIDTH // FR, (part + 1) * WIDTH // FR, load, col_min, unroll=16)
    col_min = over_groups(col_min, jnp.minimum)

    weight = jnp.exp2(-INNER * col_min)

    def first(f, total):
        e = jnp.exp2(INNER * (col_min - d_ref[f]))
        e_ref[f] = e
        a = 1.0 / jnp.sum(e * weight, 0, keepdims=True)
        return total + e * a

    zero = jnp.zeros((N, N), jnp.float32)
    b = 1.0 / over_groups(lax.fori_loop(0, FAC, first, zero, unroll=UNROLL), jnp.add)

    for _ in range(2):

        def later(f, total, b=b):
            e = e_ref[f]
            a = 1.0 / jnp.sum(e * b, 0, keepdims=True)
            a_ref[pl.ds(f, 1), :] = a
            return total + e * a

        b = 1.0 / over_groups(lax.fori_loop(0, FAC, later, zero, unroll=UNROLL), jnp.add)

    row_part = temper * jnp.log(a_ref[...])
    a_ref[...] = row_part
    col = col_min + temper * jnp.log(b)

    def slab_done(at):
        pltpu.make_async_copy(out_ref.at[at], s_ref.at[pl.ds(0, FAC * N)], sem.at[at]).wait()

    @pl.when(slab >= 2)
    def _():
        slab_done(slot)

    def ship(f):
        for s in range(LOC):
            pltpu.make_async_copy(
                out_ref.at[slot, pl.ds(f * N + s * LR, LR)],
                s_ref.at[pl.ds((f * LOC + s) * PIECE + slab * LR, LR)],
                sem.at[slot],
            ).start()

    def emit(f, carry):
        out_ref[slot, pl.ds(pl.multiple_of(f * N, N), N), :] = d_ref[f] - col - a_ref[pl.ds(f, 1), :]

        @pl.when(f > 0)
        def _():
            ship(f - 1)

        return carry

    lax.fori_loop(0, FAC, emit, 0, unroll=UNROLL)
    ship(FAC - 1)
    row = m_ref[...] + row_part
    u_ref[...] = jnp.concatenate([row, jnp.zeros((N - FAC, N), jnp.float32)], 0).T
    v_ref[...] = col.T[:LR]
    worth = over_groups(jnp.sum(row, 0, keepdims=True), jnp.add) + jnp.sum(col, 0, keepdims=True)
    w_ref[pl.ds(slab, 1), :] = worth * (1.0 / N)

    @pl.when(slab == FR - 1)
    def _():
        leader = jnp.concatenate([b_ref[...]] * LOC, 1) + w_ref[...]
        group = lax.broadcasted_iota(jnp.int32, (1, N), 1) // LR
        line = leader[:1]
        for i in range(FR):
            line = jnp.where(group == ((i + loc) & (LOC - 1)), leader[i : i + 1], line)
        line_ref[...] = line

        def send(d, carry):
            pltpu.make_async_copy(line_ref, s_ref.at[pl.ds(d * PIECE + N, 1)], line_sem).start()
            return carry

        lax.fori_loop(0, DEVICES, send, 0, unroll=8)

        pltpu.make_async_copy(out_ref.at[0, pl.ds(0, DEVICES)], s_ref.at[pl.ds(0, DEVICES)], line_sem).wait()
        slab_done(1 - slot)
        slab_done(slot)


def sweeps(quad_cost, leader):
    rows = LR * N
    return pl.pallas_call(
        sweep_kernel,
        grid=(FR,),
        in_specs=[
            pl.BlockSpec(memory_space=pl.ANY),
            pl.BlockSpec((FR, LR), lambda i: (0, 0)),
        ],
        out_specs=[
            pl.BlockSpec(memory_space=pl.ANY),
            pl.BlockSpec((None, N, N), lambda i: (i, 0, 0)),
            pl.BlockSpec((None, LR, N), lambda i: (i, 0, 0)),
        ],
        out_shape=[
            jax.ShapeDtypeStruct((DEVICES * PIECE, N), jnp.float32),
            jax.ShapeDtypeStruct((FR, N, N), jnp.float32),
            jax.ShapeDtypeStruct((FR, LR, N), jnp.float32),
        ],
        scratch_shapes=[
            pltpu.VMEM((FAC, N, N), jnp.float32),
            pltpu.VMEM((FAC, N, N), jnp.float32),
            pltpu.VMEM((FAC, N), jnp.float32),
            pltpu.VMEM((FAC, N), jnp.float32),
            pltpu.VMEM((FR, N), jnp.float32),
            pltpu.VMEM((2, LR * PITCH, N), jnp.float32),
            pltpu.VMEM((2, FAC * N, N), jnp.float32),
            pltpu.VMEM((1, N), jnp.float32),
            pltpu.SemaphoreType.DMA((2, PARTS)),
            pltpu.SemaphoreType.DMA((2,)),
            pltpu.SemaphoreType.DMA,
        ],
        compiler_params=pltpu.CompilerParams(vmem_limit_bytes=VMEM_LIMIT),
    )(quad_cost.reshape(FR * rows, N), leader)


def own_kernel(c_ref, u_ref, v_ref, o_ref):
    step = pl.program_id(0)
    loc = lax.axis_index("loc")
    c_rows = c_ref.reshape(FR * LR * STEP, N)
    o_rows = o_ref.reshape(FR * LR * STEP, N)
    for g in range(STEP_F):
        shift = lax.rem(N - (step * STEP_F + g), N)
        for k in range(FR):
            begin = ((k + loc) & (FR - 1)) * LR
            for a in range(FR):
                row = u_ref[a, pl.ds(pl.multiple_of(begin, LR), LR), :]
                row = pltpu.roll(row, shift, 1)[:, :1]
                at = pl.ds(a * LR * STEP + g * FR + k, LR, stride=STEP)
                o_rows[at, :] = 0.5 * (c_rows[at, :] - row - v_ref[a])


def own_half(quad_cost, row, col):
    return pl.pallas_call(
        own_kernel,
        grid=(N // STEP,),
        in_specs=[
            pl.BlockSpec((FR, LR, STEP, N), lambda i: (0, 0, i, 0)),
            pl.BlockSpec((FR, N, N), lambda i: (0, 0, 0)),
            pl.BlockSpec((FR, LR, N), lambda i: (0, 0, 0)),
        ],
        out_specs=pl.BlockSpec((FR, LR, STEP, N), lambda i: (0, 0, i, 0)),
        out_shape=jax.ShapeDtypeStruct((FR, LR, N, N), jnp.float32),
        compiler_params=pltpu.CompilerParams(vmem_limit_bytes=VMEM_LIMIT),
        cost_estimate=pl.CostEstimate(flops=1 << 23, bytes_accessed=1 << 24, transcendentals=0),
    )(quad_cost, row, col)


def regroup(parts):
    group = lax.broadcasted_iota(jnp.int32, parts[0].shape, 1) // LR
    odd = (group & 1) == 1
    low = group < 2
    p0, p1, p2, p3 = parts
    even_a, even_b = jnp.where(odd, p1, p0), jnp.where(odd, p3, p2)
    odd_a, odd_b = jnp.where(odd, p0, p3), jnp.where(odd, p2, p1)
    return [
        jnp.where(low, even_a, even_b),
        pltpu.roll(jnp.where(low, odd_a, odd_b), 3 * LR, 1),
        pltpu.roll(jnp.where(low, even_b, even_a), 2 * LR, 1),
        pltpu.roll(jnp.where(low, odd_b, odd_a), LR, 1),
    ]


def soft_min(values, axis, scale):
    scaled = -values / scale
    highest = jnp.max(scaled, axis=axis, keepdims=True)
    totals = jnp.sum(jnp.exp(scaled - highest), axis=axis, keepdims=True)
    return -scale * (highest + jnp.log(totals))


def join_kernel(q_ref, r_ref, o_ref, nb_ref, in_ref, lead_ref, bs_ref, sem, lead_sem):
    step = pl.program_id(0)
    slot = step & 1
    sources = STEP_F * LOC * FR

    def piece(at, n, to):
        f, g, i = n // (LOC * FR), n // FR % LOC, n % FR
        return pltpu.make_async_copy(
            r_ref.at[pl.ds(((at * STEP_F + f) * LOC + g) * PIECE + i * LR, LR)],
            in_ref.at[to, g, pl.ds((f * FR + i) * SPACE, LR)],
            sem.at[to],
        )

    def fetch(at, to):
        for n in range(sources):
            piece(at, n, to).start()

    def lead(d):
        return pltpu.make_async_copy(r_ref.at[pl.ds(d * PIECE + N, 1)], lead_ref.at[pl.ds(d, 1)], lead_sem)

    @pl.when(step == 0)
    def _():
        fetch(0, 0)

        def start(d, carry):
            lead(d).start()
            return carry

        lax.fori_loop(0, DEVICES, start, 0, unroll=8)

    @pl.when(step + 1 < pl.num_programs(0))
    def _():
        fetch(step + 1, 1 - slot)

    @pl.when(step == 1)
    def _():
        pltpu.make_async_copy(r_ref.at[pl.ds(0, DEVICES)], lead_ref, lead_sem).wait()
        fac, loc = (lax.axis_index(name) for name in AXES)
        b = regroup([lead_ref[pl.ds(g, FAC, stride=LOC), :] for g in range(LOC)])
        b = [x - soft_min(x, 1, leader_temper) for x in b]
        b = jnp.concatenate(b, 0)
        bs_ref[...] = b - soft_min(b, 0, leader_temper)
        for i in range(FR):
            row = bs_ref[pl.ds(i * FAC + fac, 1), :]
            row = pltpu.roll(row, (LOC - loc) * LR, 1)
            nb_ref[pl.ds(i, 1), :] = row[:, :LR]

    pltpu.make_async_copy(r_ref.at[pl.ds(0, sources * LR)], r_ref.at[pl.ds(0, sources * LR)], sem.at[slot]).wait()
    for t in range(STEP // 8):
        for b in range(LR):
            parts = regroup([in_ref[slot, g, pl.ds(t * 8 * SPACE + b, 8, stride=SPACE), :] for g in range(LOC)])
            for a in range(FR):
                o_ref[a, b, pl.ds(t * 8, 8), :] = q_ref[a, b, pl.ds(t * 8, 8), :] + 0.5 * parts[a]


def join(own, incoming):
    return pl.pallas_call(
        join_kernel,
        grid=(N // STEP,),
        in_specs=[
            pl.BlockSpec((FR, LR, STEP, N), lambda i: (0, 0, i, 0)),
            pl.BlockSpec(memory_space=pl.ANY),
        ],
        out_specs=[
            pl.BlockSpec((FR, LR, STEP, N), lambda i: (0, 0, i, 0)),
            pl.BlockSpec((FR, LR), lambda i: (0, 0)),
        ],
        out_shape=[
            jax.ShapeDtypeStruct((FR, LR, N, N), jnp.float32),
            jax.ShapeDtypeStruct((FR, LR), jnp.float32),
        ],
        scratch_shapes=[
            pltpu.VMEM((2, LOC, STEP * SPACE, N), jnp.float32),
            pltpu.VMEM((DEVICES, N), jnp.float32),
            pltpu.VMEM((N, N), jnp.float32),
            pltpu.SemaphoreType.DMA((2,)),
            pltpu.SemaphoreType.DMA,
        ],
        compiler_params=pltpu.CompilerParams(vmem_limit_bytes=VMEM_LIMIT),
    )(own, incoming)


def on_device(quad_cost, leader):
    send, row, col = sweeps(quad_cost, leader)
    send = send.reshape(DEVICES, PIECE, 1, N)
    incoming = lax.all_to_all(send, AXES, split_axis=0, concat_axis=0, tiled=True)
    own = own_half(quad_cost, row, col)
    return tuple(join(own, incoming.reshape(DEVICES * PIECE, N)))


def solution(mesh):
    return jax.shard_map(
        on_device,
        mesh=mesh,
        in_specs=(P("fac", "loc", None, None), P("fac", "loc")),
        out_specs=(P("fac", "loc", None, None), P("fac", "loc")),
        check_vma=False,
    )
```

```python
import jax
import jax.numpy as jnp
from jax import lax
from jax.experimental import pallas as pl
from jax.experimental.pallas import tpu as pltpu
from jax.sharding import PartitionSpec as P

N = 128
FAC = 32
LOC = 4
FR = N // FAC
LR = N // LOC

temper = 0.15
leader_temper = 0.1
LOG2E = 1.4426950408889634
INNER = LOG2E / temper
UNROLL = 32
DEVICES = FAC * LOC
PIECE = N + 1
PITCH = N + 1
PARTS = 2
WIDTH = N // PARTS
STEP = 32
STEP_F = STEP // FR
BAND = 32
SPACE = BAND + 1
VMEM_LIMIT = 67043328
AXES = ("loc", "fac")


def over_groups(x, combine):
    x = combine(x, pltpu.roll(x, LR, 1))
    return combine(x, pltpu.roll(x, 2 * LR, 1))


def sweep_kernel(c_ref, b_ref, s_ref, u_ref, v_ref, d_ref, e_ref, m_ref, a_ref, w_ref, in_ref, out_ref, line_ref, in_sem, sem, line_sem):
    slab = pl.program_id(0)
    slot = slab & 1
    loc = lax.axis_index("loc")

    def fetch(at, to):
        for part in range(PARTS):
            for j in range(LR):
                pltpu.make_async_copy(
                    c_ref.at[pl.ds((at * LR + j) * N + part * WIDTH, WIDTH)],
                    in_ref.at[to, pl.ds(j * PITCH + part * WIDTH, WIDTH)],
                    in_sem.at[to, part],
                ).start()

    @pl.when(slab == 0)
    def _():
        fetch(0, 0)

    @pl.when(slab + 1 < FR)
    def _():
        fetch(slab + 1, 1 - slot)

    def load(f, col_min):
        rows = []
        for g in range(LOC):
            k = (g + LOC - loc) & (LOC - 1)
            rows.append(in_ref[slot, pl.ds(FR * f + k, LR, stride=PITCH), :])
        x = jnp.concatenate(rows, 0).T
        row_min = jnp.min(x, 0, keepdims=True)
        x = x - row_min
        d_ref[f] = x
        m_ref[pl.ds(f, 1), :] = row_min
        return jnp.minimum(col_min, x)

    col_min = jnp.full((N, N), jnp.inf, jnp.float32)
    for part in range(PARTS):
        pltpu.make_async_copy(
            c_ref.at[pl.ds(0, LR * WIDTH)], in_ref.at[slot, pl.ds(0, LR * WIDTH)], in_sem.at[slot, part]
        ).wait()
        col_min = lax.fori_loop(part * WIDTH // FR, (part + 1) * WIDTH // FR, load, col_min, unroll=16)
    col_min = over_groups(col_min, jnp.minimum)

    weight = jnp.exp2(-INNER * col_min)

    def first(f, total):
        e = jnp.exp2(INNER * (col_min - d_ref[f]))
        e_ref[f] = e
        a = 1.0 / jnp.sum(e * weight, 0, keepdims=True)
        return total + e * a

    zero = jnp.zeros((N, N), jnp.float32)
    b = 1.0 / over_groups(lax.fori_loop(0, FAC, first, zero, unroll=UNROLL), jnp.add)

    for _ in range(2):

        def later(f, total, b=b):
            e = e_ref[f]
            a = 1.0 / jnp.sum(e * b, 0, keepdims=True)
            a_ref[pl.ds(f, 1), :] = a
            return total + e * a

        b = 1.0 / over_groups(lax.fori_loop(0, FAC, later, zero, unroll=UNROLL), jnp.add)

    row_part = temper * jnp.log(a_ref[...])
    a_ref[...] = row_part
    col = col_min + temper * jnp.log(b)

    def slab_done(at):
        pltpu.make_async_copy(out_ref.at[at], s_ref.at[pl.ds(0, FAC * N)], sem.at[at]).wait()

    @pl.when(slab >= 2)
    def _():
        slab_done(slot)

    def ship(f):
        for s in range(LOC):
            pltpu.make_async_copy(
                out_ref.at[slot, pl.ds(f * N + s * LR, LR)],
                s_ref.at[pl.ds((s * FAC + f) * PIECE + slab * LR, LR)],
                sem.at[slot],
            ).start()

    def emit(f, carry):
        out_ref[slot, pl.ds(pl.multiple_of(f * N, N), N), :] = d_ref[f] - col - a_ref[pl.ds(f, 1), :]

        @pl.when(f > 0)
        def _():
            ship(f - 1)

        return carry

    lax.fori_loop(0, FAC, emit, 0, unroll=UNROLL)
    ship(FAC - 1)
    row = m_ref[...] + row_part
    for k in range(FR):
        turn = ((LOC - k - loc) & (LOC - 1)) * LR
        u_ref[pl.ds(k, FAC, stride=FR), :] = pltpu.roll(row, turn, 1)
    v_ref[...] = col.T[:LR]
    worth = over_groups(jnp.sum(row, 0, keepdims=True), jnp.add) + jnp.sum(col, 0, keepdims=True)
    w_ref[pl.ds(slab, 1), :] = worth * (1.0 / N)

    @pl.when(slab == FR - 1)
    def _():
        leader = jnp.concatenate([b_ref[...]] * LOC, 1) + w_ref[...]
        group = lax.broadcasted_iota(jnp.int32, (1, N), 1) // LR
        line = leader[:1]
        for i in range(FR):
            line = jnp.where(group == ((i + loc) & (LOC - 1)), leader[i : i + 1], line)
        line_ref[...] = line

        def send(d, carry):
            pltpu.make_async_copy(line_ref, s_ref.at[pl.ds(d * PIECE + N, 1)], line_sem).start()
            return carry

        lax.fori_loop(0, DEVICES, send, 0, unroll=8)

        pltpu.make_async_copy(out_ref.at[0, pl.ds(0, DEVICES)], s_ref.at[pl.ds(0, DEVICES)], line_sem).wait()
        slab_done(1 - slot)
        slab_done(slot)


def sweeps(quad_cost, leader):
    rows = LR * N
    return pl.pallas_call(
        sweep_kernel,
        grid=(FR,),
        in_specs=[
            pl.BlockSpec(memory_space=pl.ANY),
            pl.BlockSpec((FR, LR), lambda i: (0, 0)),
        ],
        out_specs=[
            pl.BlockSpec(memory_space=pl.ANY),
            pl.BlockSpec((None, N, N), lambda i: (i, 0, 0)),
            pl.BlockSpec((None, LR, N), lambda i: (i, 0, 0)),
        ],
        out_shape=[
            jax.ShapeDtypeStruct((DEVICES * PIECE, N), jnp.float32),
            jax.ShapeDtypeStruct((FR, N, N), jnp.float32),
            jax.ShapeDtypeStruct((FR, LR, N), jnp.float32),
        ],
        scratch_shapes=[
            pltpu.VMEM((FAC, N, N), jnp.float32),
            pltpu.VMEM((FAC, N, N), jnp.float32),
            pltpu.VMEM((FAC, N), jnp.float32),
            pltpu.VMEM((FAC, N), jnp.float32),
            pltpu.VMEM((FR, N), jnp.float32),
            pltpu.VMEM((2, LR * PITCH, N), jnp.float32),
            pltpu.VMEM((2, FAC * N, N), jnp.float32),
            pltpu.VMEM((1, N), jnp.float32),
            pltpu.SemaphoreType.DMA((2, PARTS)),
            pltpu.SemaphoreType.DMA((2,)),
            pltpu.SemaphoreType.DMA,
        ],
        compiler_params=pltpu.CompilerParams(vmem_limit_bytes=VMEM_LIMIT),
    )(quad_cost.reshape(FR * rows, N), leader)


def regroup(parts):
    group = lax.broadcasted_iota(jnp.int32, parts[0].shape, 1) // LR
    odd = (group & 1) == 1
    low = group < 2
    p0, p1, p2, p3 = parts
    even_a, even_b = jnp.where(odd, p1, p0), jnp.where(odd, p3, p2)
    odd_a, odd_b = jnp.where(odd, p0, p3), jnp.where(odd, p2, p1)
    return [
        jnp.where(low, even_a, even_b),
        pltpu.roll(jnp.where(low, odd_a, odd_b), 3 * LR, 1),
        pltpu.roll(jnp.where(low, even_b, even_a), 2 * LR, 1),
        pltpu.roll(jnp.where(low, odd_b, odd_a), LR, 1),
    ]


def soft_min(values, axis, scale):
    scaled = -values / scale
    highest = jnp.max(scaled, axis=axis, keepdims=True)
    totals = jnp.sum(jnp.exp(scaled - highest), axis=axis, keepdims=True)
    return -scale * (highest + jnp.log(totals))


def join_kernel(c_ref, u_ref, v_ref, r_ref, o_ref, nb_ref, in_ref, lead_ref, bs_ref, sem, lead_sem):
    at = pl.program_id(0)
    band = pl.program_id(1)
    bands = LR // BAND
    step = at * bands + band
    slot = step & 1
    pieces = STEP_F * LOC * FR

    def fetch(at, band, to):
        for f in range(STEP_F):
            for g in range(LOC):
                for i in range(FR):
                    pltpu.make_async_copy(
                        r_ref.at[pl.ds((g * FAC + at * STEP_F + f) * PIECE + i * LR + band * BAND, BAND)],
                        in_ref.at[to, g, pl.ds((f * FR + i) * SPACE, BAND)],
                        sem.at[to],
                    ).start()

    def lead(d):
        return pltpu.make_async_copy(r_ref.at[pl.ds(d * PIECE + N, 1)], lead_ref.at[pl.ds(d, 1)], lead_sem)

    @pl.when(step == 0)
    def _():
        fetch(0, 0, 0)

        def start(d, carry):
            lead(d).start()
            return carry

        lax.fori_loop(0, DEVICES, start, 0, unroll=8)

    @pl.when(step + 1 < pl.num_programs(0) * bands)
    def _():
        if bands == 1:
            fetch(at + 1, 0, 1 - slot)
        else:
            wrap = band == bands - 1
            fetch(jnp.where(wrap, at + 1, at), jnp.where(wrap, 0, band + 1), 1 - slot)

    @pl.when(step == 1)
    def _():
        pltpu.make_async_copy(r_ref.at[pl.ds(0, DEVICES)], lead_ref, lead_sem).wait()
        loc, fac = (lax.axis_index(name) for name in AXES)
        b = regroup([lead_ref[pl.ds(g * FAC, FAC), :] for g in range(LOC)])
        b = [x - soft_min(x, 1, leader_temper) for x in b]
        b = jnp.concatenate(b, 0)
        bs_ref[...] = b - soft_min(b, 0, leader_temper)
        for i in range(FR):
            row = bs_ref[pl.ds(i * FAC + fac, 1), :]
            row = pltpu.roll(row, (LOC - loc) * LR, 1)
            nb_ref[pl.ds(i, 1), :] = row[:, :LR]

    pltpu.make_async_copy(r_ref.at[pl.ds(0, pieces * BAND)], r_ref.at[pl.ds(0, pieces * BAND)], sem.at[slot]).wait()
    for t in range(STEP // 8):
        rows = pl.ds(pl.multiple_of(at * STEP + t * 8, 8), 8)
        for a in range(FR):
            col = u_ref[a, rows, :]
            if bands > 1:
                col = pltpu.roll(col, (N - band * BAND) & (N - 1), 1)
            if a == 0:
                cols = []
            cols.append(col)
        for b in range(BAND):
            parts = regroup([in_ref[slot, g, pl.ds(t * 8 * SPACE + b, 8, stride=SPACE), :] for g in range(LOC)])
            for a in range(FR):
                own = c_ref[a, b, pl.ds(t * 8, 8), :] - cols[a][:, b : b + 1] - v_ref[a, pl.ds(b, 1), :]
                o_ref[a, b, pl.ds(t * 8, 8), :] = 0.5 * (own + parts[a])


def join(quad_cost, row, col, incoming):
    return pl.pallas_call(
        join_kernel,
        grid=(N // STEP, LR // BAND),
        in_specs=[
            pl.BlockSpec((FR, BAND, STEP, N), lambda i, b: (0, b, i, 0)),
            pl.BlockSpec((FR, N, N), lambda i, b: (0, 0, 0)),
            pl.BlockSpec((FR, BAND, N), lambda i, b: (0, b, 0)),
            pl.BlockSpec(memory_space=pl.ANY),
        ],
        out_specs=[
            pl.BlockSpec((FR, BAND, STEP, N), lambda i, b: (0, b, i, 0)),
            pl.BlockSpec((FR, LR), lambda i, b: (0, 0)),
        ],
        out_shape=[
            jax.ShapeDtypeStruct((FR, LR, N, N), jnp.float32),
            jax.ShapeDtypeStruct((FR, LR), jnp.float32),
        ],
        scratch_shapes=[
            pltpu.VMEM((2, LOC, STEP * SPACE, N), jnp.float32),
            pltpu.VMEM((DEVICES, N), jnp.float32),
            pltpu.VMEM((N, N), jnp.float32),
            pltpu.SemaphoreType.DMA((2,)),
            pltpu.SemaphoreType.DMA,
        ],
        compiler_params=pltpu.CompilerParams(vmem_limit_bytes=VMEM_LIMIT),
    )(quad_cost, row, col, incoming)


def on_device(quad_cost, leader):
    send, row, col = sweeps(quad_cost, leader)
    send = send.reshape(DEVICES, PIECE, 1, N)
    incoming = lax.all_to_all(send, AXES, split_axis=0, concat_axis=0, tiled=True)
    return tuple(join(quad_cost, row, col, incoming.reshape(DEVICES * PIECE, N)))


def solution(mesh):
    return jax.shard_map(
        on_device,
        mesh=mesh,
        in_specs=(P("fac", "loc", None, None), P("fac", "loc")),
        out_specs=(P("fac", "loc", None, None), P("fac", "loc")),
        check_vma=False,
    )
```

```python
import jax
import jax.numpy as jnp
from jax import lax
from jax.experimental import pallas as pl
from jax.experimental.pallas import tpu as pltpu
from jax.sharding import PartitionSpec as P

N = 128
FAC = 32
LOC = 4
FR = N // FAC
LR = N // LOC

temper = 0.15
leader_temper = 0.1
LOG2E = 1.4426950408889634
INNER = LOG2E / temper
UNROLL = 32
DEVICES = FAC * LOC
PIECE = N + 1
PITCH = N + 1
PARTS = 2
WIDTH = N // PARTS
STEP = 32
STEP_F = STEP // FR
BAND = 32
SPACE = BAND + 1
VMEM_LIMIT = 67043328
JOIN_LIMIT = 40 << 20
AXES = ("loc", "fac")


def over_groups(x, combine):
    x = combine(x, pltpu.roll(x, LR, 1))
    return combine(x, pltpu.roll(x, 2 * LR, 1))


def sweep_kernel(c_ref, b_ref, s_ref, u_ref, v_ref, d_ref, e_ref, m_ref, a_ref, w_ref, in_ref, out_ref, line_ref, in_sem, sem, line_sem):
    slab = pl.program_id(0)
    slot = slab & 1
    loc = lax.axis_index("loc")

    def fetch(at, to):
        for part in range(PARTS):
            for j in range(LR):
                pltpu.make_async_copy(
                    c_ref.at[pl.ds((at * LR + j) * N + part * WIDTH, WIDTH)],
                    in_ref.at[to, pl.ds(j * PITCH + part * WIDTH, WIDTH)],
                    in_sem.at[to, part],
                ).start()

    @pl.when(slab == 0)
    def _():
        fetch(0, 0)

    @pl.when(slab + 1 < FR)
    def _():
        fetch(slab + 1, 1 - slot)

    def load(f, col_min):
        rows = []
        for g in range(LOC):
            k = (g + LOC - loc) & (LOC - 1)
            rows.append(in_ref[slot, pl.ds(FR * f + k, LR, stride=PITCH), :])
        x = jnp.concatenate(rows, 0).T
        row_min = jnp.min(x, 0, keepdims=True)
        x = x - row_min
        d_ref[f] = x
        m_ref[pl.ds(f, 1), :] = row_min
        return jnp.minimum(col_min, x)

    col_min = jnp.full((N, N), jnp.inf, jnp.float32)
    for part in range(PARTS):
        pltpu.make_async_copy(
            c_ref.at[pl.ds(0, LR * WIDTH)], in_ref.at[slot, pl.ds(0, LR * WIDTH)], in_sem.at[slot, part]
        ).wait()
        col_min = lax.fori_loop(part * WIDTH // FR, (part + 1) * WIDTH // FR, load, col_min, unroll=16)
    col_min = over_groups(col_min, jnp.minimum)

    weight = jnp.exp2(-INNER * col_min)

    def first(f, total):
        e = jnp.exp2(INNER * (col_min - d_ref[f]))
        e_ref[f] = e
        a = 1.0 / jnp.sum(e * weight, 0, keepdims=True)
        return total + e * a

    zero = jnp.zeros((N, N), jnp.float32)
    b = 1.0 / over_groups(lax.fori_loop(0, FAC, first, zero, unroll=UNROLL), jnp.add)

    for _ in range(2):

        def later(f, total, b=b):
            e = e_ref[f]
            a = 1.0 / jnp.sum(e * b, 0, keepdims=True)
            a_ref[pl.ds(f, 1), :] = a
            return total + e * a

        b = 1.0 / over_groups(lax.fori_loop(0, FAC, later, zero, unroll=UNROLL), jnp.add)

    row_part = temper * jnp.log(a_ref[...])
    a_ref[...] = row_part
    col = col_min + temper * jnp.log(b)

    def slab_done(at):
        pltpu.make_async_copy(out_ref.at[at], s_ref.at[pl.ds(0, FAC * N)], sem.at[at]).wait()

    @pl.when(slab >= 2)
    def _():
        slab_done(slot)

    def ship(f):
        for s in range(LOC):
            pltpu.make_async_copy(
                out_ref.at[slot, pl.ds(f * N + s * LR, LR)],
                s_ref.at[pl.ds((s * FAC + f) * PIECE + slab * LR, LR)],
                sem.at[slot],
            ).start()

    def emit(f, carry):
        out_ref[slot, pl.ds(pl.multiple_of(f * N, N), N), :] = d_ref[f] - col - a_ref[pl.ds(f, 1), :]

        @pl.when(f > 0)
        def _():
            ship(f - 1)

        return carry

    lax.fori_loop(0, FAC, emit, 0, unroll=UNROLL)
    ship(FAC - 1)
    row = m_ref[...] + row_part
    for k in range(FR):
        turn = ((LOC - k - loc) & (LOC - 1)) * LR
        u_ref[pl.ds(k, FAC, stride=FR), :] = pltpu.roll(row, turn, 1)
    v_ref[...] = col.T[:LR]
    worth = over_groups(jnp.sum(row, 0, keepdims=True), jnp.add) + jnp.sum(col, 0, keepdims=True)
    w_ref[pl.ds(slab, 1), :] = worth * (1.0 / N)

    @pl.when(slab == FR - 1)
    def _():
        leader = jnp.concatenate([b_ref[...]] * LOC, 1) + w_ref[...]
        group = lax.broadcasted_iota(jnp.int32, (1, N), 1) // LR
        line = leader[:1]
        for i in range(FR):
            line = jnp.where(group == ((i + loc) & (LOC - 1)), leader[i : i + 1], line)
        line_ref[...] = line

        def send(d, carry):
            pltpu.make_async_copy(line_ref, s_ref.at[pl.ds(d * PIECE + N, 1)], line_sem).start()
            return carry

        lax.fori_loop(0, DEVICES, send, 0, unroll=8)

        pltpu.make_async_copy(out_ref.at[0, pl.ds(0, DEVICES)], s_ref.at[pl.ds(0, DEVICES)], line_sem).wait()
        slab_done(1 - slot)
        slab_done(slot)


def sweeps(quad_cost, leader):
    rows = LR * N
    return pl.pallas_call(
        sweep_kernel,
        grid=(FR,),
        in_specs=[
            pl.BlockSpec(memory_space=pl.ANY),
            pl.BlockSpec((FR, LR), lambda i: (0, 0)),
        ],
        out_specs=[
            pl.BlockSpec(memory_space=pl.ANY),
            pl.BlockSpec((None, N, N), lambda i: (i, 0, 0)),
            pl.BlockSpec((None, LR, N), lambda i: (i, 0, 0)),
        ],
        out_shape=[
            jax.ShapeDtypeStruct((DEVICES * PIECE, N), jnp.float32),
            jax.ShapeDtypeStruct((FR, N, N), jnp.float32),
            jax.ShapeDtypeStruct((FR, LR, N), jnp.float32),
        ],
        scratch_shapes=[
            pltpu.VMEM((FAC, N, N), jnp.float32),
            pltpu.VMEM((FAC, N, N), jnp.float32),
            pltpu.VMEM((FAC, N), jnp.float32),
            pltpu.VMEM((FAC, N), jnp.float32),
            pltpu.VMEM((FR, N), jnp.float32),
            pltpu.VMEM((2, LR * PITCH, N), jnp.float32),
            pltpu.VMEM((2, FAC * N, N), jnp.float32),
            pltpu.VMEM((1, N), jnp.float32),
            pltpu.SemaphoreType.DMA((2, PARTS)),
            pltpu.SemaphoreType.DMA((2,)),
            pltpu.SemaphoreType.DMA,
        ],
        compiler_params=pltpu.CompilerParams(vmem_limit_bytes=VMEM_LIMIT),
    )(quad_cost.reshape(FR * rows, N), leader)


def regroup(parts):
    group = lax.broadcasted_iota(jnp.int32, parts[0].shape, 1) // LR
    odd = (group & 1) == 1
    low = group < 2
    p0, p1, p2, p3 = parts
    even_a, even_b = jnp.where(odd, p1, p0), jnp.where(odd, p3, p2)
    odd_a, odd_b = jnp.where(odd, p0, p3), jnp.where(odd, p2, p1)
    return [
        jnp.where(low, even_a, even_b),
        pltpu.roll(jnp.where(low, odd_a, odd_b), 3 * LR, 1),
        pltpu.roll(jnp.where(low, even_b, even_a), 2 * LR, 1),
        pltpu.roll(jnp.where(low, odd_b, odd_a), LR, 1),
    ]


def soft_min(values, axis, scale):
    scaled = -values / scale
    highest = jnp.max(scaled, axis=axis, keepdims=True)
    totals = jnp.sum(jnp.exp(scaled - highest), axis=axis, keepdims=True)
    return -scale * (highest + jnp.log(totals))


def join_kernel(c_ref, u_ref, v_ref, r_ref, o_ref, nb_ref, in_ref, lead_ref, bs_ref, sem, lead_sem):
    at = pl.program_id(0)
    band = pl.program_id(1)
    bands = LR // BAND
    step = at * bands + band
    slot = step & 1
    pieces = STEP_F * LOC * FR

    def fetch(at, band, to):
        for f in range(STEP_F):
            for g in range(LOC):
                for i in range(FR):
                    pltpu.make_async_copy(
                        r_ref.at[pl.ds((g * FAC + at * STEP_F + f) * PIECE + i * LR + band * BAND, BAND)],
                        in_ref.at[to, g, pl.ds((f * FR + i) * SPACE, BAND)],
                        sem.at[to],
                    ).start()

    def lead(d):
        return pltpu.make_async_copy(r_ref.at[pl.ds(d * PIECE + N, 1)], lead_ref.at[pl.ds(d, 1)], lead_sem)

    @pl.when(step == 0)
    def _():
        fetch(0, 0, 0)

        def start(d, carry):
            lead(d).start()
            return carry

        lax.fori_loop(0, DEVICES, start, 0, unroll=8)

    @pl.when(step + 1 < pl.num_programs(0) * bands)
    def _():
        if bands == 1:
            fetch(at + 1, 0, 1 - slot)
        else:
            wrap = band == bands - 1
            fetch(jnp.where(wrap, at + 1, at), jnp.where(wrap, 0, band + 1), 1 - slot)

    @pl.when(step == 1)
    def _():
        pltpu.make_async_copy(r_ref.at[pl.ds(0, DEVICES)], lead_ref, lead_sem).wait()
        loc, fac = (lax.axis_index(name) for name in AXES)
        b = regroup([lead_ref[pl.ds(g * FAC, FAC), :] for g in range(LOC)])
        b = [x - soft_min(x, 1, leader_temper) for x in b]
        b = jnp.concatenate(b, 0)
        bs_ref[...] = b - soft_min(b, 0, leader_temper)
        for i in range(FR):
            row = bs_ref[pl.ds(i * FAC + fac, 1), :]
            row = pltpu.roll(row, (LOC - loc) * LR, 1)
            nb_ref[pl.ds(i, 1), :] = row[:, :LR]

    pltpu.make_async_copy(r_ref.at[pl.ds(0, pieces * BAND)], r_ref.at[pl.ds(0, pieces * BAND)], sem.at[slot]).wait()
    for t in range(STEP // 8):
        rows = pl.ds(pl.multiple_of(at * STEP + t * 8, 8), 8)
        for a in range(FR):
            col = u_ref[a, rows, :]
            if bands > 1:
                col = pltpu.roll(col, (N - band * BAND) & (N - 1), 1)
            if a == 0:
                cols = []
            cols.append(col)
        for b in range(BAND):
            parts = regroup([in_ref[slot, g, pl.ds(t * 8 * SPACE + b, 8, stride=SPACE), :] for g in range(LOC)])
            for a in range(FR):
                own = c_ref[a, b, rows, :] - cols[a][:, b : b + 1] - v_ref[a, pl.ds(b, 1), :]
                o_ref[a, b, pl.ds(t * 8, 8), :] = 0.5 * (own + parts[a])


def join(quad_cost, row, col, incoming):
    return pl.pallas_call(
        join_kernel,
        grid=(N // STEP, LR // BAND),
        in_specs=[
            pl.BlockSpec(memory_space=pltpu.VMEM),
            pl.BlockSpec((FR, N, N), lambda i, b: (0, 0, 0)),
            pl.BlockSpec((FR, BAND, N), lambda i, b: (0, b, 0)),
            pl.BlockSpec(memory_space=pl.ANY),
        ],
        out_specs=[
            pl.BlockSpec((FR, BAND, STEP, N), lambda i, b: (0, b, i, 0)),
            pl.BlockSpec((FR, LR), lambda i, b: (0, 0)),
        ],
        out_shape=[
            jax.ShapeDtypeStruct((FR, LR, N, N), jnp.float32),
            jax.ShapeDtypeStruct((FR, LR), jnp.float32),
        ],
        scratch_shapes=[
            pltpu.VMEM((2, LOC, STEP * SPACE, N), jnp.float32),
            pltpu.VMEM((DEVICES, N), jnp.float32),
            pltpu.VMEM((N, N), jnp.float32),
            pltpu.SemaphoreType.DMA((2,)),
            pltpu.SemaphoreType.DMA,
        ],
        compiler_params=pltpu.CompilerParams(vmem_limit_bytes=JOIN_LIMIT),
    )(quad_cost, row, col, incoming)


def on_device(quad_cost, leader):
    send, row, col = sweeps(quad_cost, leader)
    send = send.reshape(DEVICES, PIECE, 1, N)
    incoming = lax.all_to_all(send, AXES, split_axis=0, concat_axis=0, tiled=True)
    return tuple(join(quad_cost, row, col, incoming.reshape(DEVICES * PIECE, N)))


def solution(mesh):
    return jax.shard_map(
        on_device,
        mesh=mesh,
        in_specs=(P("fac", "loc", None, None), P("fac", "loc")),
        out_specs=(P("fac", "loc", None, None), P("fac", "loc")),
        check_vma=False,
    )
```

```python
import jax
import jax.numpy as jnp
from jax import lax
from jax.experimental import pallas as pl
from jax.experimental.pallas import tpu as pltpu
from jax.sharding import PartitionSpec as P

N = 128
FAC = 32
LOC = 4
FR = N // FAC
LR = N // LOC

temper = 0.15
leader_temper = 0.1
LOG2E = 1.4426950408889634
INNER = LOG2E / temper
UNROLL = 32
DEVICES = FAC * LOC
PIECE = N + 1
PITCH = N + 1
PARTS = 2
WIDTH = N // PARTS
STEP = 32
STEP_F = STEP // FR
BAND = 32
SPACE = BAND + 1
VMEM_LIMIT = 67043328
JOIN_LIMIT = 40 << 20
AXES = ("loc", "fac")


def over_groups(x, combine):
    x = combine(x, pltpu.roll(x, LR, 1))
    return combine(x, pltpu.roll(x, 2 * LR, 1))


def sweep_kernel(c_ref, b_ref, s_ref, u_ref, v_ref, d_ref, e_ref, m_ref, a_ref, w_ref, in_ref, out_ref, line_ref, in_sem, sem, line_sem):
    slab = pl.program_id(0)
    slot = slab & 1
    loc = lax.axis_index("loc")

    def fetch(at, to):
        for part in range(PARTS):
            for j in range(LR):
                pltpu.make_async_copy(
                    c_ref.at[pl.ds((at * LR + j) * N + part * WIDTH, WIDTH)],
                    in_ref.at[to, pl.ds(j * PITCH + part * WIDTH, WIDTH)],
                    in_sem.at[to, part],
                ).start()

    @pl.when(slab == 0)
    def _():
        fetch(0, 0)

    @pl.when(slab + 1 < FR)
    def _():
        fetch(slab + 1, 1 - slot)

    def load(f, col_min):
        rows = []
        for g in range(LOC):
            k = (g + LOC - loc) & (LOC - 1)
            rows.append(in_ref[slot, pl.ds(FR * f + k, LR, stride=PITCH), :])
        x = jnp.concatenate(rows, 0).T
        row_min = jnp.min(x, 0, keepdims=True)
        x = x - row_min
        d_ref[f] = x
        m_ref[pl.ds(f, 1), :] = row_min
        return jnp.minimum(col_min, x)

    col_min = jnp.full((N, N), jnp.inf, jnp.float32)
    for part in range(PARTS):
        pltpu.make_async_copy(
            c_ref.at[pl.ds(0, LR * WIDTH)], in_ref.at[slot, pl.ds(0, LR * WIDTH)], in_sem.at[slot, part]
        ).wait()
        col_min = lax.fori_loop(part * WIDTH // FR, (part + 1) * WIDTH // FR, load, col_min, unroll=16)
    col_min = over_groups(col_min, jnp.minimum)

    weight = jnp.exp2(-INNER * col_min)

    def first(f, total):
        e = jnp.exp2(INNER * (col_min - d_ref[f]))
        e_ref[f] = e
        a = 1.0 / jnp.sum(e * weight, 0, keepdims=True)
        return total + e * a

    zero = jnp.zeros((N, N), jnp.float32)
    b = 1.0 / over_groups(lax.fori_loop(0, FAC, first, zero, unroll=UNROLL), jnp.add)

    for _ in range(2):

        def later(f, total, b=b):
            e = e_ref[f]
            a = 1.0 / jnp.sum(e * b, 0, keepdims=True)
            a_ref[pl.ds(f, 1), :] = a
            return total + e * a

        b = 1.0 / over_groups(lax.fori_loop(0, FAC, later, zero, unroll=UNROLL), jnp.add)

    row_part = temper * jnp.log(a_ref[...])
    a_ref[...] = row_part
    col = col_min + temper * jnp.log(b)

    def slab_done(at):
        pltpu.make_async_copy(out_ref.at[at], s_ref.at[pl.ds(0, FAC * N)], sem.at[at]).wait()

    @pl.when(slab >= 2)
    def _():
        slab_done(slot)

    def ship(f):
        for s in range(LOC):
            pltpu.make_async_copy(
                out_ref.at[slot, pl.ds(f * N + s * LR, LR)],
                s_ref.at[pl.ds((s * FAC + f) * PIECE + slab * LR, LR)],
                sem.at[slot],
            ).start()

    row = m_ref[...] + row_part
    for k in range(FR):
        turn = ((LOC - k - loc) & (LOC - 1)) * LR
        u_ref[pl.ds(k, FAC, stride=FR), :] = pltpu.roll(row, turn, 1)
    v_ref[...] = col.T[:LR]
    worth = over_groups(jnp.sum(row, 0, keepdims=True), jnp.add) + jnp.sum(col, 0, keepdims=True)
    w_ref[pl.ds(slab, 1), :] = worth * (1.0 / N)

    @pl.when(slab == FR - 1)
    def _():
        leader = jnp.concatenate([b_ref[...]] * LOC, 1) + w_ref[...]
        group = lax.broadcasted_iota(jnp.int32, (1, N), 1) // LR
        line = leader[:1]
        for i in range(FR):
            line = jnp.where(group == ((i + loc) & (LOC - 1)), leader[i : i + 1], line)
        line_ref[...] = line

        def send(d, carry):
            pltpu.make_async_copy(line_ref, s_ref.at[pl.ds(d * PIECE + N, 1)], line_sem).start()
            return carry

        lax.fori_loop(0, DEVICES, send, 0, unroll=8)


    def emit(f, carry):
        out_ref[slot, pl.ds(pl.multiple_of(f * N, N), N), :] = d_ref[f] - col - a_ref[pl.ds(f, 1), :]

        @pl.when(f > 0)
        def _():
            ship(f - 1)

        return carry

    lax.fori_loop(0, FAC, emit, 0, unroll=UNROLL)
    ship(FAC - 1)

    @pl.when(slab == FR - 1)
    def _():
        pltpu.make_async_copy(out_ref.at[0, pl.ds(0, DEVICES)], s_ref.at[pl.ds(0, DEVICES)], line_sem).wait()
        slab_done(1 - slot)
        slab_done(slot)


def sweeps(quad_cost, leader):
    rows = LR * N
    return pl.pallas_call(
        sweep_kernel,
        grid=(FR,),
        in_specs=[
            pl.BlockSpec(memory_space=pl.ANY),
            pl.BlockSpec((FR, LR), lambda i: (0, 0)),
        ],
        out_specs=[
            pl.BlockSpec(memory_space=pl.ANY),
            pl.BlockSpec((None, N, N), lambda i: (i, 0, 0)),
            pl.BlockSpec((None, LR, N), lambda i: (i, 0, 0)),
        ],
        out_shape=[
            jax.ShapeDtypeStruct((DEVICES * PIECE, N), jnp.float32),
            jax.ShapeDtypeStruct((FR, N, N), jnp.float32),
            jax.ShapeDtypeStruct((FR, LR, N), jnp.float32),
        ],
        scratch_shapes=[
            pltpu.VMEM((FAC, N, N), jnp.float32),
            pltpu.VMEM((FAC, N, N), jnp.float32),
            pltpu.VMEM((FAC, N), jnp.float32),
            pltpu.VMEM((FAC, N), jnp.float32),
            pltpu.VMEM((FR, N), jnp.float32),
            pltpu.VMEM((2, LR * PITCH, N), jnp.float32),
            pltpu.VMEM((2, FAC * N, N), jnp.float32),
            pltpu.VMEM((1, N), jnp.float32),
            pltpu.SemaphoreType.DMA((2, PARTS)),
            pltpu.SemaphoreType.DMA((2,)),
            pltpu.SemaphoreType.DMA,
        ],
        compiler_params=pltpu.CompilerParams(vmem_limit_bytes=VMEM_LIMIT),
    )(quad_cost.reshape(FR * rows, N), leader)


def regroup(parts):
    group = lax.broadcasted_iota(jnp.int32, parts[0].shape, 1) // LR
    odd = (group & 1) == 1
    low = group < 2
    p0, p1, p2, p3 = parts
    even_a, even_b = jnp.where(odd, p1, p0), jnp.where(odd, p3, p2)
    odd_a, odd_b = jnp.where(odd, p0, p3), jnp.where(odd, p2, p1)
    return [
        jnp.where(low, even_a, even_b),
        pltpu.roll(jnp.where(low, odd_a, odd_b), 3 * LR, 1),
        pltpu.roll(jnp.where(low, even_b, even_a), 2 * LR, 1),
        pltpu.roll(jnp.where(low, odd_b, odd_a), LR, 1),
    ]


def soft_min(values, axis, scale):
    scaled = -values / scale
    highest = jnp.max(scaled, axis=axis, keepdims=True)
    totals = jnp.sum(jnp.exp(scaled - highest), axis=axis, keepdims=True)
    return -scale * (highest + jnp.log(totals))


def join_kernel(c_ref, u_ref, v_ref, r_ref, o_ref, nb_ref, in_ref, lead_ref, bs_ref, sem, lead_sem):
    at = pl.program_id(0)
    band = pl.program_id(1)
    bands = LR // BAND
    step = at * bands + band
    slot = step & 1
    pieces = STEP_F * LOC * FR

    def fetch(at, band, to):
        for f in range(STEP_F):
            for g in range(LOC):
                for i in range(FR):
                    pltpu.make_async_copy(
                        r_ref.at[pl.ds((g * FAC + at * STEP_F + f) * PIECE + i * LR + band * BAND, BAND)],
                        in_ref.at[to, g, pl.ds((f * FR + i) * SPACE, BAND)],
                        sem.at[to],
                    ).start()

    def lead(d):
        return pltpu.make_async_copy(r_ref.at[pl.ds(d * PIECE + N, 1)], lead_ref.at[pl.ds(d, 1)], lead_sem)

    @pl.when(step == 0)
    def _():
        fetch(0, 0, 0)

        def start(d, carry):
            lead(d).start()
            return carry

        lax.fori_loop(0, DEVICES, start, 0, unroll=8)

    @pl.when(step + 1 < pl.num_programs(0) * bands)
    def _():
        if bands == 1:
            fetch(at + 1, 0, 1 - slot)
        else:
            wrap = band == bands - 1
            fetch(jnp.where(wrap, at + 1, at), jnp.where(wrap, 0, band + 1), 1 - slot)

    @pl.when(step == 1)
    def _():
        pltpu.make_async_copy(r_ref.at[pl.ds(0, DEVICES)], lead_ref, lead_sem).wait()
        loc, fac = (lax.axis_index(name) for name in AXES)
        b = regroup([lead_ref[pl.ds(g * FAC, FAC), :] for g in range(LOC)])
        b = [x - soft_min(x, 1, leader_temper) for x in b]
        b = jnp.concatenate(b, 0)
        bs_ref[...] = b - soft_min(b, 0, leader_temper)
        for i in range(FR):
            row = bs_ref[pl.ds(i * FAC + fac, 1), :]
            row = pltpu.roll(row, (LOC - loc) * LR, 1)
            nb_ref[pl.ds(i, 1), :] = row[:, :LR]

    pltpu.make_async_copy(r_ref.at[pl.ds(0, pieces * BAND)], r_ref.at[pl.ds(0, pieces * BAND)], sem.at[slot]).wait()
    for t in range(STEP // 8):
        rows = pl.ds(pl.multiple_of(at * STEP + t * 8, 8), 8)
        for a in range(FR):
            col = u_ref[a, rows, :]
            if bands > 1:
                col = pltpu.roll(col, (N - band * BAND) & (N - 1), 1)
            if a == 0:
                cols = []
            cols.append(col)
        for b in range(BAND):
            parts = regroup([in_ref[slot, g, pl.ds(t * 8 * SPACE + b, 8, stride=SPACE), :] for g in range(LOC)])
            for a in range(FR):
                own = c_ref[a, b, rows, :] - cols[a][:, b : b + 1] - v_ref[a, pl.ds(b, 1), :]
                o_ref[a, b, pl.ds(t * 8, 8), :] = 0.5 * (own + parts[a])


def join(quad_cost, row, col, incoming):
    return pl.pallas_call(
        join_kernel,
        grid=(N // STEP, LR // BAND),
        in_specs=[
            pl.BlockSpec(memory_space=pltpu.VMEM),
            pl.BlockSpec((FR, N, N), lambda i, b: (0, 0, 0)),
            pl.BlockSpec((FR, BAND, N), lambda i, b: (0, b, 0)),
            pl.BlockSpec(memory_space=pl.ANY),
        ],
        out_specs=[
            pl.BlockSpec((FR, BAND, STEP, N), lambda i, b: (0, b, i, 0)),
            pl.BlockSpec((FR, LR), lambda i, b: (0, 0)),
        ],
        out_shape=[
            jax.ShapeDtypeStruct((FR, LR, N, N), jnp.float32),
            jax.ShapeDtypeStruct((FR, LR), jnp.float32),
        ],
        scratch_shapes=[
            pltpu.VMEM((2, LOC, STEP * SPACE, N), jnp.float32),
            pltpu.VMEM((DEVICES, N), jnp.float32),
            pltpu.VMEM((N, N), jnp.float32),
            pltpu.SemaphoreType.DMA((2,)),
            pltpu.SemaphoreType.DMA,
        ],
        compiler_params=pltpu.CompilerParams(vmem_limit_bytes=JOIN_LIMIT),
    )(quad_cost, row, col, incoming)


def on_device(quad_cost, leader):
    send, row, col = sweeps(quad_cost, leader)
    send = send.reshape(DEVICES, PIECE, 1, N)
    incoming = lax.all_to_all(send, AXES, split_axis=0, concat_axis=0, tiled=True)
    return tuple(join(quad_cost, row, col, incoming.reshape(DEVICES * PIECE, N)))


def solution(mesh):
    return jax.shard_map(
        on_device,
        mesh=mesh,
        in_specs=(P("fac", "loc", None, None), P("fac", "loc")),
        out_specs=(P("fac", "loc", None, None), P("fac", "loc")),
        check_vma=False,
    )
```
